256 devices in a mesh: ia: 8 (over z_lo, y), ib: 8 (over z_hi, core), op: 4 (over x).
Axes of the slice: x: 4, y: 4, z: 8 (z_hi: 4, z_lo: 2; z = z_hi * 2 + z_lo), core: 2. Of those that a mesh axis runs over, the one named last changes fastest.
Arguments:
- fit_coefficients: bfloat16 [8, 3072, 4096], P('ia', ('ib', 'op')), may hold values from -0.09375 to 0.09375
- three_center: bfloat16 [4, 4096, 3072], P(None, None, ('ib', 'op')), may hold values from -6 to 6
- amplitudes: bfloat16 [32, 3072, 3072], P('op', ('ia', 'ib')), may hold values from -0.001953125 to 0.001953125
- pair_list: int32 [32, 2], P('op'), may hold values from 0 to 255
- slot_tiles: int32 [64], replicated, may hold values from 0 to 63, each once
- energy_occupied: float32 [256], replicated, may hold values from -1.2 to -0.4
- energy_left: float32 [8], P('ia'), may hold values from 0.3 to 2.5
- energy_right: float32 [4], replicated, may hold values from 0.3 to 2.5
Outputs:
- update: float32 [32, 8, 4], P('op', 'ia')
The draws below stay inside these ranges and needn't reach their ends.
Inputs may be any that keep to these rules, and one draw needn't show every extreme that they name: `slot_tiles`: each tile number stands in exactly one slot.
All inputs are finite; a program needn't handle non-finite values.
Results may differ from the reference program's by a relative error of at most 0.0029.
Values may be sent and summed in bfloat16 or wider, within the bound.
No kernel may reach another device: no remote copies, remote signals or barrier semaphores. Data moves between devices by JAX's collectives and lax.ppermute only.
A program may use at most 128 MiB of HBM per device.

```python
import jax
import jax.numpy as jnp
from jax import lax

V = 3072
NAUX = 4096
NOCC = 256
PAIRS = 32
NA = 8
NB = 4
NTILE = 64
TW = 48


def place_ends(values, own_key, least, largest):
    extent = values.shape
    place = [jax.random.randint(jax.random.fold_in(own_key, axis), (), 0, extent[axis]) for axis in range(len(extent))]
    values = values.at[tuple(place)].set(least)
    longest = extent.index(max(extent))
    place[longest] = (place[longest] + 1) % extent[longest]
    return values.at[tuple(place)].set(largest)


def levels(rng, shape, shards, low, high):
    level = 1.0
    for dim, parts in shards:
        draws = jax.random.uniform(jax.random.fold_in(jax.random.fold_in(rng, 6), dim), (parts,), jnp.float32, low / len(shards), high / len(shards))
        level = level * jnp.repeat(jnp.exp(draws), shape[dim] // parts).reshape((-1,) + (1,) * (len(shape) - 1 - dim))
    return level


def scatter_about(stream_key, shape, deviation, limit, cuts=(), held_as=jnp.bfloat16):
    factor_of = levels(stream_key, shape, cuts, -0.22, 0.18) if cuts else 1.0
    result = jax.random.normal(stream_key, shape, jnp.float32) * deviation * factor_of
    return jnp.minimum(jnp.maximum(result, -limit), limit).astype(held_as)


def setup_inputs(seed: int = 0) -> dict:
    key_of = jax.random.split(jax.random.key(seed), 9)
    fit_coefficients = scatter_about(key_of[0], (NA, V, NAUX), NAUX ** -0.5, 0.09375, ((0, 8), (1, 32)))
    three_center = scatter_about(key_of[1], (NB, NAUX, V), 1.0, 6.0, ((2, 32),))
    amplitudes = scatter_about(key_of[2], (PAIRS, V, V), (V * V) ** -0.5, 0.001953125, ((0, 4), (1, 64)))
    pair_list = place_ends(jax.random.randint(key_of[3], (PAIRS, 2), 0, NOCC), jax.random.fold_in(key_of[3], 1), 0, NOCC - 1).astype(jnp.int32)
    slot_tiles = jax.random.permutation(key_of[4], NTILE).astype(jnp.int32)
    energy_occupied = jnp.clip(jax.random.uniform(key_of[5], (NOCC,), jnp.float32, -1.2, -0.4), -1.2, -0.4)
    energy_left = jnp.clip(0.3 + 2.2 * jax.random.uniform(key_of[6], (NA,), jnp.float32) ** levels(key_of[6], (NA,), ((0, 8),), -0.2, 0.2), 0.3, 2.5)
    energy_right = jnp.clip(jax.random.uniform(key_of[7], (NB,), jnp.float32, 0.3, 2.5), 0.3, 2.5)
    return dict(fit_coefficients=fit_coefficients, three_center=three_center, amplitudes=amplitudes, pair_list=pair_list, slot_tiles=slot_tiles, energy_occupied=energy_occupied, energy_left=energy_left, energy_right=energy_right)


laplace_points = (0.06, 0.25, 0.7, 1.6, 3.5)
laplace_weights = (0.16, 0.36, 0.62, 1.0, 1.7)


def reference(fit_coefficients, three_center, amplitudes, pair_list, slot_tiles, energy_occupied, energy_left, energy_right):
    flat_amplitudes = amplitudes.reshape(PAIRS, V * V)

    def one_entry(position):
        left_index = position // NB
        right_index = position % NB
        fit_row = lax.dynamic_index_in_dim(fit_coefficients, left_index, 0, keepdims=False)
        center_row = lax.dynamic_index_in_dim(three_center, right_index, 0, keepdims=False)
        integrals = jnp.dot(fit_row, center_row, preferred_element_type=jnp.float32).astype(jnp.bfloat16)
        integrals = integrals.reshape(NTILE, TW, V)[slot_tiles].reshape(V * V)
        return jnp.dot(flat_amplitudes, integrals, preferred_element_type=jnp.float32)

    residual = lax.map(one_entry, jnp.arange(NA * NB, dtype=jnp.int32))
    residual = jnp.transpose(residual).reshape(PAIRS, NA, NB)
    occupied_sum = energy_occupied[pair_list[:, 0]] + energy_occupied[pair_list[:, 1]]
    denominator = energy_left[None, :, None] + energy_right[None, None, :] - occupied_sum[:, None, None]
    factor = jnp.zeros_like(denominator)
    for point, weight in zip(laplace_points, laplace_weights):
        factor = factor + weight * jnp.exp(-point * denominator)
    return residual * factor
```

```python
import jax
import jax.numpy as jnp
from jax import lax
from jax.sharding import PartitionSpec as P

laplace_points = (0.06, 0.25, 0.7, 1.6, 3.5)
laplace_weights = (0.16, 0.36, 0.62, 1.0, 1.7)


def laplace_factor(pair_list, energy_occupied, energy_left, energy_right):
    occupied = energy_occupied.shape[0]
    column = lax.broadcasted_iota(jnp.int32, (pair_list.shape[0], occupied), 1)
    first = jnp.sum(jnp.where(pair_list[:, 0:1] == column, energy_occupied[None, :], 0.0), axis=1)
    second = jnp.sum(jnp.where(pair_list[:, 1:2] == column, energy_occupied[None, :], 0.0), axis=1)
    denominator = (
        energy_left[None, :, None]
        + energy_right[None, None, :]
        - (first + second)[:, None, None]
    )
    factor = jnp.zeros_like(denominator)
    for point, weight in zip(laplace_points, laplace_weights):
        factor = factor + weight * jnp.exp(-point * denominator)
    return factor


def reduce_to_owner(partial_value, local_pairs):
    total_pairs, left, right = partial_value.shape
    groups = total_pairs // local_pairs
    pieces = partial_value.reshape(groups, local_pairs, left, right)
    pieces = pieces.transpose(2, 0, 1, 3).reshape(left * groups, 1, local_pairs * right)
    pieces = lax.all_to_all(pieces, ("ia", "op"), split_axis=0, concat_axis=0, tiled=True)
    mine = jnp.sum(pieces, axis=0, keepdims=True)
    spread = lax.axis_size("ib")
    copies = jnp.broadcast_to(mine, (spread, 1, local_pairs * right))
    copies = lax.all_to_all(copies, "ib", split_axis=0, concat_axis=0, tiled=True)
    return jnp.sum(copies, axis=0).reshape(local_pairs, 1, right)


def per_device(
    fit_coefficients,
    three_center,
    amplitudes,
    pair_list,
    slot_tiles,
    energy_occupied,
    energy_left,
    energy_right,
):
    right_rows = three_center.shape[0]
    share = three_center.shape[2]
    tile_width = amplitudes.shape[1]
    local_pairs = amplitudes.shape[0]
    left_count = lax.axis_size("ia")
    right_count = lax.axis_size("ib")
    group_count = lax.axis_size("op")
    slot_count = left_count * right_count
    total_pairs = local_pairs * group_count

    gathered = lax.all_gather(fit_coefficients, ("ib", "op"), axis=1, tiled=True)[0]

    split_amps = amplitudes.reshape(local_pairs, tile_width, right_count * group_count, share)
    split_amps = split_amps.transpose(2, 1, 0, 3)
    amps = lax.all_to_all(split_amps, ("ib", "op"), split_axis=0, concat_axis=0, tiled=True)
    amps = amps.reshape(right_count, group_count, tile_width, local_pairs, share)

    integrals = jnp.einsum(
        "cq,bqd->bcd", gathered, three_center, preferred_element_type=jnp.float32
    ).astype(jnp.bfloat16)
    tiles = integrals.reshape(right_rows, slot_count, tile_width, share)
    ordered = tiles.at[:, slot_tiles].get(mode="promise_in_bounds")
    arrived = lax.all_to_all(ordered, "ia", split_axis=1, concat_axis=0, tiled=True)
    arrived = arrived.reshape(left_count, right_rows, right_count, tile_width, share)
    partial_value = jnp.einsum(
        "sgkpe,abske->gpab", amps, arrived, preferred_element_type=jnp.float32
    ).reshape(total_pairs, left_count, right_rows)

    owned = reduce_to_owner(partial_value, local_pairs)
    return owned * laplace_factor(pair_list, energy_occupied, energy_left, energy_right)


def solution(mesh):
    placed = (
        P("ia", ("ib", "op"), None),
        P(None, None, ("ib", "op")),
        P("op", ("ia", "ib"), None),
        P("op", None),
        P(),
        P(),
        P("ia"),
        P(),
    )
    return jax.shard_map(
        per_device, mesh=mesh, in_specs=placed, out_specs=P("op", "ia", None), check_vma=False
    )
```

```python
import jax
import jax.numpy as jnp
from jax import lax
from jax.sharding import Mesh
from jax.sharding import PartitionSpec as P


laplace_points = (0.06, 0.25, 0.7, 1.6, 3.5)
laplace_weights = (0.16, 0.36, 0.62, 1.0, 1.7)


def laplace_factor(pair_list, energy_occupied, energy_left, energy_right):
    occupied = energy_occupied.shape[0]
    column = lax.broadcasted_iota(jnp.int32, (pair_list.shape[0], occupied), 1)
    first = jnp.sum(jnp.where(pair_list[:, 0:1] == column, energy_occupied[None, :], 0.0), axis=1)
    second = jnp.sum(jnp.where(pair_list[:, 1:2] == column, energy_occupied[None, :], 0.0), axis=1)
    denominator = (
        energy_left[None, :, None]
        + energy_right[None, None, :]
        - (first + second)[:, None, None]
    )
    factor = jnp.zeros_like(denominator)
    for point, weight in zip(laplace_points, laplace_weights):
        factor = factor + weight * jnp.exp(-point * denominator)
    return factor


def reduce_to_owner(partial_value, local_pairs):
    total_pairs, left, right = partial_value.shape
    groups = total_pairs // local_pairs
    spread = lax.axis_size(("zh", "k"))
    pieces = partial_value.reshape(groups, local_pairs, left, right)
    pieces = pieces.transpose(2, 0, 1, 3).reshape(left, 1, groups, local_pairs * right)
    pieces = jnp.broadcast_to(pieces, (left, spread, groups, local_pairs * right))
    pieces = pieces.reshape(left * spread * groups, local_pairs * right)
    pieces = lax.all_to_all(
        pieces, ("ia", "zh", "k", "op"), split_axis=0, concat_axis=0, tiled=True
    )
    return jnp.sum(pieces, axis=0).reshape(local_pairs, 1, right)


def shift(value, axis, step):
    size = lax.axis_size(axis)
    return lax.ppermute(value, axis, [(i, (i + step) % size) for i in range(size)])


def ring_halves(block, axis):
    half = block.shape[0] // 2
    up = shift(block, axis, 1)
    down = shift(block, axis, -1)
    far0 = shift(up[:half], axis, 1)
    far1 = shift(down[half:], axis, -1)
    return up, down, jnp.concatenate([far0, far1], axis=0)


def per_device(
    fit_coefficients,
    three_center,
    amplitudes,
    pair_list,
    slot_tiles,
    energy_occupied,
    energy_left,
    energy_right,
):
    right_rows = three_center.shape[0]
    share = three_center.shape[2]
    naux = three_center.shape[1]
    tile_width = amplitudes.shape[1]
    local_pairs = amplitudes.shape[0]
    left_count = lax.axis_size("ia")
    high_count = lax.axis_size("zh")
    core_count = lax.axis_size("k")
    group_count = lax.axis_size("op")
    right_count = high_count * core_count
    slot_count = left_count * right_count
    total_pairs = local_pairs * group_count

    own = fit_coefficients[0]
    rows = own.shape[0]
    below, above, opposite = ring_halves(own, "zh")
    columns = three_center.transpose(0, 2, 1).reshape(right_rows * share, naux)
    columns_other = shift(columns, "k", 1)

    blocks0 = (own,) + ring_halves(own, "op")
    blocks1 = (jnp.concatenate([below, above], axis=0),)
    blocks1 = blocks1 + ring_halves(blocks1[0], "op")
    blocks2 = (opposite,) + ring_halves(opposite, "op")

    split_amps = amplitudes.reshape(local_pairs, tile_width, right_count, group_count, share)
    split_amps = split_amps.transpose(2, 3, 1, 0, 4)
    split_amps = split_amps.reshape(
        right_count, group_count, tile_width, local_pairs * share
    )
    split_amps, _ = lax.optimization_barrier((split_amps, opposite))
    amps = lax.all_to_all(
        split_amps, ("zh", "k"), split_axis=0, concat_axis=0, tiled=True
    )
    amps = lax.all_to_all(amps, "op", split_axis=1, concat_axis=1, tiled=True)
    amps = amps.reshape(right_count, group_count, tile_width, local_pairs, share)
    amps = amps.transpose(1, 3, 2, 0, 4).reshape(total_pairs, tile_width, right_count, share)

    kept, sent = [], []
    for blocks in (blocks0, blocks1, blocks2):
        block = jnp.concatenate(blocks, axis=0)
        for weights, out in ((columns, kept), (columns_other, sent)):
            product = lax.dot_general(
                block,
                weights,
                (((1,), (1,)), ((), ())),
                preferred_element_type=jnp.float32,
            )
            out.append(product.astype(jnp.bfloat16))
    swapped = [shift(value, "k", 1) for value in sent]
    stacked = jnp.concatenate(kept + swapped, axis=0)
    stacked = stacked.reshape(slot_count, tile_width, right_rows * share)

    def ring_place(source, axis):
        step = (source - lax.axis_index(axis)) % 4
        return jnp.where(step == 0, 0, jnp.where(step == 3, 1, step + 1))

    per_block = rows // tile_width
    block_of = slot_tiles // per_block
    across = ring_place(block_of % group_count, "op")
    core = (block_of // group_count) % core_count
    up = ring_place(block_of // (group_count * core_count), "zh")
    position = jnp.where(
        up == 0,
        across,
        jnp.where(
            up == 3,
            3 * group_count + across,
            group_count + 2 * across + (up - 1),
        ),
    )
    swap = jnp.where(core == lax.axis_index("k"), 0, high_count * group_count)
    place = (position + swap) * per_block + slot_tiles % per_block
    ordered = stacked.at[place].get(mode="promise_in_bounds")
    arrived = lax.all_to_all(ordered, "ia", split_axis=0, concat_axis=0, tiled=True)
    arrived = arrived.reshape(left_count, right_count, tile_width, right_rows, share)
    partial_value = jnp.einsum("pkse,askbe->pab", amps, arrived, preferred_element_type=jnp.float32)

    owned = reduce_to_owner(partial_value, local_pairs)
    return owned * laplace_factor(pair_list, energy_occupied, energy_left, energy_right)


def solution(mesh):
    sizes = mesh.shape
    cores = 2
    devices = mesh.devices.reshape(sizes["ia"], sizes["ib"] // cores, cores, sizes["op"])
    fine = Mesh(devices, ("ia", "zh", "k", "op"))
    placed = (
        P("ia", ("zh", "k", "op"), None),
        P(None, None, ("zh", "k", "op")),
        P("op", ("ia", "zh", "k"), None),
        P("op", None),
        P(),
        P(),
        P("ia"),
        P(),
    )
    return jax.shard_map(
        per_device, mesh=fine, in_specs=placed, out_specs=P("op", "ia", None), check_vma=False
    )
```

```python
import jax
import jax.numpy as jnp
from jax import lax
from jax.sharding import Mesh
from jax.sharding import PartitionSpec as P
from jax.experimental import pallas as pl
from jax.experimental.pallas import tpu as pltpu


laplace_points = (0.06, 0.25, 0.7, 1.6, 3.5)
laplace_weights = (0.16, 0.36, 0.62, 1.0, 1.7)


def laplace_factor(pair_list, energy_occupied, energy_left, energy_right):
    occupied = energy_occupied.shape[0]
    column = lax.broadcasted_iota(jnp.int32, (pair_list.shape[0], occupied), 1)
    first = jnp.sum(jnp.where(pair_list[:, 0:1] == column, energy_occupied[None, :], 0.0), axis=1)
    second = jnp.sum(jnp.where(pair_list[:, 1:2] == column, energy_occupied[None, :], 0.0), axis=1)
    denominator = (
        energy_left[None, :, None]
        + energy_right[None, None, :]
        - (first + second)[:, None, None]
    )
    factor = jnp.zeros_like(denominator)
    for point, weight in zip(laplace_points, laplace_weights):
        factor = factor + weight * jnp.exp(-point * denominator)
    return factor


def shift(value, axis, step):
    size = lax.axis_size(axis)
    return lax.ppermute(value, axis, [(i, (i + step) % size) for i in range(size)])


def ring_halves(block, axis):
    half = block.shape[0] // 2
    up = shift(block, axis, 1)
    down = shift(block, axis, -1)
    far0 = shift(up[:half], axis, 1)
    far1 = shift(down[half:], axis, -1)
    return [up, down, far0, far1]


def ring_whole(block, axis, step):
    up = shift(block, axis, 1)
    down = shift(block, axis, -1)
    far = shift(up if step > 0 else down, axis, step)
    return [up, down, far]


def contract_last(left, right):
    return lax.dot_general(
        left, right, (((1,), (1,)), ((), ())), preferred_element_type=jnp.float32
    )


def group_products(pieces, columns, stacks, kept_shape, sent_shape, row):
    count = len(pieces)
    total = sum(piece.shape[0] for piece in pieces)
    both, depth = columns.shape
    width = both // 2
    step = 1024
    steps = depth // step

    def body(*refs):
        rows, weights = refs[:count], refs[count]
        kept, sent, acc = refs[-3:]
        index = pl.program_id(0)
        left = jnp.concatenate([ref[...] for ref in rows], axis=0)
        product = contract_last(left, weights[...])

        @pl.when(index == 0)
        def _():
            acc[...] = product

        @pl.when((index > 0) & (index < steps - 1))
        def _():
            acc[...] += product

        @pl.when(index == steps - 1)
        def _():
            result = (acc[...] + product).astype(kept.dtype)
            kept[...] = result[:, :width]
            sent[...] = result[:, width:]

    in_specs = [pl.BlockSpec((piece.shape[0], step), lambda k: (0, k)) for piece in pieces]
    in_specs.append(pl.BlockSpec((both, step), lambda k: (0, k)))
    aliases = {}
    carried = []
    for position, stack in enumerate(stacks):
        if stack is not None:
            aliases[count + 1 + len(carried)] = position
            carried.append(stack)
            in_specs.append(pl.BlockSpec(memory_space=pl.ANY))
    sent_row = row if sent_shape[0] > total else 0
    return pl.pallas_call(
        body,
        grid=(steps,),
        in_specs=in_specs,
        out_specs=[
            pl.BlockSpec((total, width), lambda k: (row, 0)),
            pl.BlockSpec((total, width), lambda k: (sent_row, 0)),
        ],
        out_shape=[
            jax.ShapeDtypeStruct(kept_shape, columns.dtype),
            jax.ShapeDtypeStruct(sent_shape, columns.dtype),
        ],
        scratch_shapes=[pltpu.VMEM((total, both), jnp.float32)],
        input_output_aliases=aliases,
        cost_estimate=pl.CostEstimate(
            flops=2 * total * both * depth,
            transcendentals=0,
            bytes_accessed=2 * depth * (total + both) + 2 * total * both,
        ),
    )(*pieces, columns, *carried)


LANE = 128
CHUNK = 16


def lane_window(values, start, share):
    first = start // LANE * LANE
    shift_by = start - first
    low = values[:, first : first + LANE]
    if shift_by == 0:
        return low
    low = pltpu.roll(low, LANE - shift_by, 1)
    if shift_by + share <= LANE:
        return low
    high = pltpu.roll(values[:, first + LANE : first + 2 * LANE], LANE - shift_by, 1)
    place = lax.broadcasted_iota(jnp.int32, low.shape, 1)
    return jnp.where(place < LANE - shift_by, low, high)


def amplitude_rows(pieces, share):
    groups = len(pieces)
    slots, width, lanes_in = pieces[0].shape
    local_pairs = lanes_in // share
    chunks = width // CHUNK
    rows = local_pairs * groups * CHUNK

    def body(*refs):
        in_refs, out_ref = refs[:groups], refs[groups]
        for part in range(chunks):
            span = slice(part * CHUNK, (part + 1) * CHUNK)
            block = jnp.concatenate([ref[0, span, :] for ref in in_refs], axis=0)
            block = block.astype(jnp.float32)
            live = lax.broadcasted_iota(jnp.int32, (groups * CHUNK, LANE), 1) < share
            for p in range(local_pairs):
                piece = jnp.where(live, lane_window(block, p * share, share), 0.0)
                out_ref[
                    0,
                    p * groups * CHUNK : (p + 1) * groups * CHUNK,
                    part * LANE : (part + 1) * LANE,
                ] = piece.astype(out_ref.dtype)

    return pl.pallas_call(
        body,
        grid=(slots,),
        in_specs=[pl.BlockSpec((1, width, lanes_in), lambda i: (i, 0, 0))] * groups,
        out_specs=pl.BlockSpec((1, rows, chunks * LANE), lambda i: (i // 2, 0, i % 2)),
        out_shape=jax.ShapeDtypeStruct(
            (slots // 2, rows, 2 * chunks * LANE), pieces[0].dtype
        ),
        name="amprows",
    )(*pieces)


def pair_sums(arrived, amp_rows, group, right_rows, groups):
    left_count, slots, width, _ = arrived.shape
    share = arrived.shape[3] // right_rows
    steps, columns, depth = amp_rows.shape
    local_pairs = columns // (groups * CHUNK)
    chunks = width // CHUNK
    block_rows = left_count * CHUNK
    rows = right_rows * block_rows
    lanes = groups * local_pairs * right_rows

    def body(group_ref, left_ref, right_ref, out_ref, acc):
        index = pl.program_id(0)
        parts = []
        for slot in range(2):
            for part in range(chunks):
                span = slice(part * CHUNK, (part + 1) * CHUNK)
                block = left_ref[:, slot, span, :].astype(jnp.float32)
                block = block.reshape(block_rows, right_rows * share)
                parts.append(
                    jnp.concatenate(
                        [
                            lane_window(block, b * share, share).astype(jnp.bfloat16)
                            for b in range(right_rows)
                        ],
                        axis=0,
                    )
                )
        product = contract_last(jnp.concatenate(parts, axis=1), right_ref[0])

        @pl.when(index == 0)
        def _():
            acc[...] = product

        @pl.when(index > 0)
        def _():
            acc[...] += product

        @pl.when(index == steps - 1)
        def _():
            row_c = lax.broadcasted_iota(jnp.int32, (rows, columns), 0) % CHUNK
            column_c = lax.broadcasted_iota(jnp.int32, (rows, columns), 1) % CHUNK
            diagonal = jnp.where(row_c == column_c, acc[...], 0.0)
            diagonal = jnp.sum(diagonal.reshape(rows // CHUNK, CHUNK, columns), axis=1)
            source = lax.broadcasted_iota(jnp.int32, (columns, lanes), 0) // CHUNK
            target = lax.broadcasted_iota(jnp.int32, (columns, lanes), 1)
            owner = (group_ref[0] + groups - source % groups) % groups
            first = (owner * local_pairs + source // groups) * right_rows
            select = jnp.where(target // right_rows * right_rows == first, 1.0, 0.0)
            spread = jnp.dot(
                diagonal,
                select,
                precision=lax.Precision.HIGHEST,
                preferred_element_type=jnp.float32,
            )
            lane_b = lax.broadcasted_iota(jnp.int32, (left_count, lanes), 1) % right_rows
            total = jnp.zeros((left_count, lanes), jnp.float32)
            for b in range(right_rows):
                mine = spread[b * left_count : (b + 1) * left_count, :]
                total = jnp.where(lane_b == b, mine, total)
            out_ref[...] = jnp.broadcast_to(total[:, None, :], out_ref.shape)

    return pl.pallas_call(
        body,
        grid_spec=pltpu.PrefetchScalarGridSpec(
            num_scalar_prefetch=1,
            grid=(steps,),
            in_specs=[
                pl.BlockSpec((left_count, 2, width, right_rows * share), lambda i, _: (0, i, 0, 0)),
                pl.BlockSpec((1, columns, depth), lambda i, _: (i, 0, 0)),
            ],
            out_specs=pl.BlockSpec((left_count, slots, lanes), lambda i, _: (0, 0, 0)),
            scratch_shapes=[pltpu.VMEM((rows, columns), jnp.float32)],
        ),
        out_shape=jax.ShapeDtypeStruct((left_count, slots, lanes), jnp.float32),
        name="pairsums",
    )(group.reshape(1), pltpu.with_memory_space_constraint(arrived, pltpu.HBM), amp_rows)


def reduce_to_owner(sums, local_pairs):
    left = sums.shape[0]
    groups = lax.axis_size("op")
    spread = lax.axis_size(("zh", "k"))
    owned = sums.shape[2] // groups
    pieces = sums.reshape(left * spread * groups, owned)
    pieces = lax.all_to_all(
        pieces, ("ia", "zh", "k", "op"), split_axis=0, concat_axis=0, tiled=True
    )
    return jnp.sum(pieces, axis=0).reshape(local_pairs, 1, owned // local_pairs)


def per_device(
    fit_coefficients,
    three_center,
    amplitudes,
    pair_list,
    slot_tiles,
    energy_occupied,
    energy_left,
    energy_right,
):
    right_rows = three_center.shape[0]
    share = three_center.shape[2]
    naux = three_center.shape[1]
    tile_width = amplitudes.shape[1]
    local_pairs = amplitudes.shape[0]
    left_count = lax.axis_size("ia")
    high_count = lax.axis_size("zh")
    core_count = lax.axis_size("k")
    group_count = lax.axis_size("op")
    right_count = high_count * core_count
    slot_count = left_count * right_count

    own = fit_coefficients[0]
    rows = own.shape[0]
    below, above, opposite0, opposite1 = ring_halves(own, "zh")
    columns = three_center.transpose(0, 2, 1).reshape(right_rows * share, naux)
    columns_other = shift(columns, "k", 1)
    columns_both = jnp.concatenate([columns, columns_other], axis=0)
    opposite = jnp.concatenate([opposite0, opposite1], axis=0)

    pieces0 = [own] + ring_halves(own, "op")
    pieces1 = [below] + ring_whole(below, "op", 1)
    pieces1 += [above] + ring_whole(above, "op", -1)
    pieces2 = [opposite] + ring_halves(opposite, "op")

    split_amps = amplitudes.reshape(local_pairs, tile_width, right_count, group_count, share)
    split_amps = split_amps.transpose(2, 3, 1, 0, 4)
    split_amps = split_amps.reshape(right_count, group_count, tile_width, local_pairs * share)
    amps = lax.all_to_all(
        split_amps, ("zh", "k"), split_axis=0, concat_axis=0, tiled=True
    )
    group = lax.axis_index("op")

    def for_step(step):
        to = (group + step) & (group_count - 1)
        return lax.dynamic_index_in_dim(amps, to, axis=1, keepdims=False)

    amp_pieces = [for_step(0)]
    for step in range(1, group_count):
        amp_pieces.append(shift(for_step(step), "op", step))

    ring = group_count * rows
    kept_shape = (high_count * ring, right_rows * share)
    first_shape = (3 * ring, right_rows * share)
    last_shape = (ring, right_rows * share)
    kept, sent = group_products(pieces0, columns_both, (None, None), kept_shape, first_shape, 2)
    kept, sent = group_products(pieces1, columns_both, (kept, sent), kept_shape, first_shape, 0)
    kept, sent_last = group_products(pieces2, columns_both, (kept, None), kept_shape, last_shape, 3)
    swapped = [shift(sent, "k", 1), shift(sent_last, "k", 1)]
    stacked = jnp.concatenate([kept] + swapped, axis=0)
    stacked = stacked.reshape(slot_count, tile_width, right_rows * share)

    per_block = rows // tile_width
    block_of = slot_tiles // per_block
    step = (block_of % group_count - lax.axis_index("op")) % group_count
    across = jnp.where(step == 0, 0, jnp.where(step == 3, 1, step + 1))
    core = (block_of // group_count) % core_count
    step = (block_of // (group_count * core_count) - lax.axis_index("zh")) % high_count
    up = jnp.where(step == 0, 2, jnp.where(step == 3, 0, jnp.where(step == 1, 1, 3)))
    swap = jnp.where(core == lax.axis_index("k"), 0, high_count)
    place = ((swap + up) * group_count + across) * per_block + slot_tiles % per_block
    ordered = stacked.at[place].get(mode="promise_in_bounds")
    arrived = lax.all_to_all(ordered, "ia", split_axis=0, concat_axis=0, tiled=True)
    arrived = arrived.reshape(left_count, right_count, tile_width, right_rows * share)
    amp_rows = amplitude_rows(amp_pieces, share)
    sums = pair_sums(arrived, amp_rows, group, right_rows, group_count)
    owned = reduce_to_owner(sums, local_pairs)
    return owned * laplace_factor(pair_list, energy_occupied, energy_left, energy_right)


def solution(mesh):
    sizes = mesh.shape
    cores = 2
    devices = mesh.devices.reshape(sizes["ia"], sizes["ib"] // cores, cores, sizes["op"])
    fine = Mesh(devices, ("ia", "zh", "k", "op"))
    placed = (
        P("ia", ("zh", "k", "op"), None),
        P(None, None, ("zh", "k", "op")),
        P("op", ("ia", "zh", "k"), None),
        P("op", None),
        P(),
        P(),
        P("ia"),
        P(),
    )
    return jax.shard_map(
        per_device, mesh=fine, in_specs=placed, out_specs=P("op", "ia", None), check_vma=False
    )
```

```python
import jax
import jax.numpy as jnp
from jax import lax
from jax.sharding import Mesh
from jax.sharding import PartitionSpec as P
from jax.experimental import pallas as pl
from jax.experimental.pallas import tpu as pltpu


laplace_points = (0.06, 0.25, 0.7, 1.6, 3.5)
laplace_weights = (0.16, 0.36, 0.62, 1.0, 1.7)


def laplace_factor(pair_list, energy_occupied, energy_left, energy_right):
    occupied = energy_occupied.shape[0]
    column = lax.broadcasted_iota(jnp.int32, (pair_list.shape[0], occupied), 1)
    first = jnp.sum(jnp.where(pair_list[:, 0:1] == column, energy_occupied[None, :], 0.0), axis=1)
    second = jnp.sum(jnp.where(pair_list[:, 1:2] == column, energy_occupied[None, :], 0.0), axis=1)
    denominator = (
        energy_left[None, :, None]
        + energy_right[None, None, :]
        - (first + second)[:, None, None]
    )
    factor = jnp.zeros_like(denominator)
    for point, weight in zip(laplace_points, laplace_weights):
        factor = factor + weight * jnp.exp(-point * denominator)
    return factor


def shift(value, axis, step):
    size = lax.axis_size(axis)
    return lax.ppermute(value, axis, [(i, (i + step) % size) for i in range(size)])


def ring_halves(block, axis):
    half = block.shape[0] // 2
    up = shift(block, axis, 1)
    down = shift(block, axis, -1)
    far0 = shift(up[:half], axis, 1)
    far1 = shift(down[half:], axis, -1)
    return [up, down, far0, far1]


def ring_whole(block, axis, step):
    up = shift(block, axis, 1)
    down = shift(block, axis, -1)
    far = shift(up if step > 0 else down, axis, step)
    return [up, down, far]


def ring_split(first, second, axis):
    up0 = shift(first, axis, 1)
    down1 = shift(second, axis, -1)
    up1 = shift(second, axis, 1)
    down0 = shift(first, axis, -1)
    far0 = shift(up0, axis, 1)
    far1 = shift(down1, axis, -1)
    return [up0, up1, down0, down1, far0, far1]


def contract_last(left, right):
    return lax.dot_general(
        left, right, (((1,), (1,)), ((), ())), preferred_element_type=jnp.float32
    )


def group_products(pieces, columns, stacks, kept_shape, sent_shape, row):
    count = len(pieces)
    total = sum(piece.shape[0] for piece in pieces)
    both, depth = columns.shape
    width = both // 2
    step = 1024
    steps = depth // step

    def body(*refs):
        rows, weights = refs[:count], refs[count]
        kept, sent, acc = refs[-3:]
        index = pl.program_id(0)
        left = jnp.concatenate([ref[...] for ref in rows], axis=0)
        product = contract_last(left, weights[...])

        @pl.when(index == 0)
        def _():
            acc[...] = product

        @pl.when((index > 0) & (index < steps - 1))
        def _():
            acc[...] += product

        @pl.when(index == steps - 1)
        def _():
            result = (acc[...] + product).astype(kept.dtype)
            kept[...] = result[:, :width]
            sent[...] = result[:, width:]

    in_specs = [pl.BlockSpec((piece.shape[0], step), lambda k: (0, k)) for piece in pieces]
    in_specs.append(pl.BlockSpec((both, step), lambda k: (0, k)))
    aliases = {}
    carried = []
    for position, stack in enumerate(stacks):
        if stack is not None:
            aliases[count + 1 + len(carried)] = position
            carried.append(stack)
            in_specs.append(pl.BlockSpec(memory_space=pl.ANY))
    sent_row = row if sent_shape[0] > total else 0
    return pl.pallas_call(
        body,
        grid=(steps,),
        in_specs=in_specs,
        out_specs=[
            pl.BlockSpec((total, width), lambda k: (row, 0)),
            pl.BlockSpec((total, width), lambda k: (sent_row, 0)),
        ],
        out_shape=[
            jax.ShapeDtypeStruct(kept_shape, columns.dtype),
            jax.ShapeDtypeStruct(sent_shape, columns.dtype),
        ],
        scratch_shapes=[pltpu.VMEM((total, both), jnp.float32)],
        input_output_aliases=aliases,
        cost_estimate=pl.CostEstimate(
            flops=2 * total * both * depth,
            transcendentals=0,
            bytes_accessed=2 * depth * (total + both) + 2 * total * both,
        ),
    )(*pieces, columns, *carried)


LANE = 128
CHUNK = 16


def lane_window(values, start, share):
    first = start // LANE * LANE
    shift_by = start - first
    low = values[:, first : first + LANE]
    if shift_by == 0:
        return low
    low = pltpu.roll(low, LANE - shift_by, 1)
    if shift_by + share <= LANE:
        return low
    high = pltpu.roll(values[:, first + LANE : first + 2 * LANE], LANE - shift_by, 1)
    place = lax.broadcasted_iota(jnp.int32, low.shape, 1)
    return jnp.where(place < LANE - shift_by, low, high)


def amplitude_rows(pieces, share):
    groups = len(pieces)
    slots, width, lanes_in = pieces[0].shape
    local_pairs = lanes_in // share
    chunks = width // CHUNK
    rows = local_pairs * groups * CHUNK

    def body(*refs):
        in_refs, out_ref = refs[:groups], refs[groups]
        for part in range(chunks):
            span = slice(part * CHUNK, (part + 1) * CHUNK)
            block = jnp.concatenate([ref[0, span, :] for ref in in_refs], axis=0)
            block = block.astype(jnp.float32)
            live = lax.broadcasted_iota(jnp.int32, (groups * CHUNK, LANE), 1) < share
            for p in range(local_pairs):
                piece = jnp.where(live, lane_window(block, p * share, share), 0.0)
                out_ref[
                    0,
                    p * groups * CHUNK : (p + 1) * groups * CHUNK,
                    part * LANE : (part + 1) * LANE,
                ] = piece.astype(out_ref.dtype)

    return pl.pallas_call(
        body,
        grid=(slots,),
        in_specs=[pl.BlockSpec((1, width, lanes_in), lambda i: (i, 0, 0))] * groups,
        out_specs=pl.BlockSpec((1, rows, chunks * LANE), lambda i: (i // 2, 0, i % 2)),
        out_shape=jax.ShapeDtypeStruct(
            (slots // 2, rows, 2 * chunks * LANE), pieces[0].dtype
        ),
        name="amprows",
    )(*pieces)


def pair_sums(arrived, amp_rows, group, right_rows, groups):
    left_count, slots, width, _ = arrived.shape
    share = arrived.shape[3] // right_rows
    steps, columns, depth = amp_rows.shape
    local_pairs = columns // (groups * CHUNK)
    chunks = width // CHUNK
    block_rows = left_count * CHUNK
    rows = right_rows * block_rows
    lanes = groups * local_pairs * right_rows

    def body(group_ref, left_ref, right_ref, out_ref, acc):
        index = pl.program_id(0)
        parts = []
        for slot in range(2):
            for part in range(chunks):
                span = slice(part * CHUNK, (part + 1) * CHUNK)
                block = left_ref[:, 2 * index + slot, span, :].astype(jnp.float32)
                block = block.reshape(block_rows, right_rows * share)
                parts.append(
                    jnp.concatenate(
                        [
                            lane_window(block, b * share, share).astype(jnp.bfloat16)
                            for b in range(right_rows)
                        ],
                        axis=0,
                    )
                )
        product = contract_last(jnp.concatenate(parts, axis=1), right_ref[0])

        @pl.when(index == 0)
        def _():
            acc[...] = product

        @pl.when(index > 0)
        def _():
            acc[...] += product

        @pl.when(index == steps - 1)
        def _():
            row_c = lax.broadcasted_iota(jnp.int32, (rows, columns), 0) % CHUNK
            column_c = lax.broadcasted_iota(jnp.int32, (rows, columns), 1) % CHUNK
            diagonal = jnp.where(row_c == column_c, acc[...], 0.0)
            diagonal = jnp.sum(diagonal.reshape(rows // CHUNK, CHUNK, columns), axis=1)
            source = lax.broadcasted_iota(jnp.int32, (columns, lanes), 0) // CHUNK
            target = lax.broadcasted_iota(jnp.int32, (columns, lanes), 1)
            owner = (group_ref[0] + groups - source % groups) % groups
            first = (owner * local_pairs + source // groups) * right_rows
            select = jnp.where(target // right_rows * right_rows == first, 1.0, 0.0)
            spread = jnp.dot(
                diagonal,
                select,
                precision=lax.Precision.HIGHEST,
                preferred_element_type=jnp.float32,
            )
            lane_b = lax.broadcasted_iota(jnp.int32, (left_count, lanes), 1) % right_rows
            total = jnp.zeros((left_count, lanes), jnp.float32)
            for b in range(right_rows):
                mine = spread[b * left_count : (b + 1) * left_count, :]
                total = jnp.where(lane_b == b, mine, total)
            owned = lanes // groups
            for g in range(groups):
                piece = total[:, g * owned : (g + 1) * owned]
                for a in range(left_count):
                    for copy in range(slots):
                        out_ref[(a * slots + copy) * groups + g] = piece[a : a + 1, :]

    return pl.pallas_call(
        body,
        grid_spec=pltpu.PrefetchScalarGridSpec(
            num_scalar_prefetch=1,
            grid=(steps,),
            in_specs=[
                pl.BlockSpec(memory_space=pltpu.VMEM),
                pl.BlockSpec((1, columns, depth), lambda i, _: (i, 0, 0)),
            ],
            out_specs=pl.BlockSpec(
                (left_count * slots * groups, 1, lanes // groups), lambda i, _: (0, 0, 0)
            ),
            scratch_shapes=[pltpu.VMEM((rows, columns), jnp.float32)],
        ),
        out_shape=jax.ShapeDtypeStruct(
            (left_count * slots * groups, 1, lanes // groups), jnp.float32
        ),
        name="pairsums",
    )(group.reshape(1), arrived, amp_rows)


def reduce_to_owner(pieces, local_pairs):
    pieces = lax.all_to_all(
        pieces, ("ia", "zh", "k", "op"), split_axis=0, concat_axis=0, tiled=True
    )
    return jnp.sum(pieces, axis=0).reshape(local_pairs, 1, -1)


def per_device(
    fit_coefficients,
    three_center,
    amplitudes,
    pair_list,
    slot_tiles,
    energy_occupied,
    energy_left,
    energy_right,
):
    right_rows = three_center.shape[0]
    share = three_center.shape[2]
    naux = three_center.shape[1]
    tile_width = amplitudes.shape[1]
    local_pairs = amplitudes.shape[0]
    left_count = lax.axis_size("ia")
    high_count = lax.axis_size("zh")
    core_count = lax.axis_size("k")
    group_count = lax.axis_size("op")
    right_count = high_count * core_count
    slot_count = left_count * right_count

    own = fit_coefficients[0]
    rows = own.shape[0]
    below, above, opposite0, opposite1 = ring_halves(own, "zh")
    columns = three_center.transpose(0, 2, 1).reshape(right_rows * share, naux)
    columns_other = shift(columns, "k", 1)
    columns_both = jnp.concatenate([columns, columns_other], axis=0)

    pieces0 = [own] + ring_halves(own, "op")
    pieces1 = [below] + ring_whole(below, "op", 1)
    pieces1 += [above] + ring_whole(above, "op", -1)
    pieces2 = [opposite0, opposite1] + ring_split(opposite0, opposite1, "op")

    split_amps = amplitudes.reshape(local_pairs, tile_width, right_count, group_count, share)
    split_amps = split_amps.transpose(2, 3, 1, 0, 4)
    split_amps = split_amps.reshape(right_count, group_count, tile_width, local_pairs * share)
    amps = lax.all_to_all(
        split_amps, ("zh", "k"), split_axis=0, concat_axis=0, tiled=True
    )
    group = lax.axis_index("op")

    def for_step(step):
        to = (group + step) & (group_count - 1)
        return lax.dynamic_index_in_dim(amps, to, axis=1, keepdims=False)

    amp_pieces = [for_step(0)]
    for step in range(1, group_count):
        amp_pieces.append(shift(for_step(step), "op", step))

    ring = group_count * rows
    kept_shape = (high_count * ring, right_rows * share)
    first_shape = (high_count * ring - rows, right_rows * share)
    last_shape = (rows, right_rows * share)
    kept, sent = group_products(pieces0, columns_both, (None, None), kept_shape, first_shape, 2)
    kept, sent = group_products(pieces1, columns_both, (kept, sent), kept_shape, first_shape, 0)
    kept, sent = group_products(
        pieces2[:-2], columns_both, (kept, sent), kept_shape, first_shape, 4
    )
    kept, sent_last = group_products(
        pieces2[-2:], columns_both, (kept, None), kept_shape, last_shape, 15
    )
    swapped = [shift(sent, "k", 1), shift(sent_last, "k", 1)]
    stacked = jnp.concatenate([kept] + swapped, axis=0)
    stacked = stacked.reshape(slot_count, tile_width, right_rows * share)

    per_block = rows // tile_width
    block_of = slot_tiles // per_block
    step = (block_of % group_count - lax.axis_index("op")) % group_count
    across = jnp.where(step == 0, 0, jnp.where(step == 3, 1, step + 1))
    core = (block_of // group_count) % core_count
    step = (block_of // (group_count * core_count) - lax.axis_index("zh")) % high_count
    up = jnp.where(step == 0, 2, jnp.where(step == 3, 0, jnp.where(step == 1, 1, 3)))
    swap = jnp.where(core == lax.axis_index("k"), 0, high_count)
    place = ((swap + up) * group_count + across) * per_block + slot_tiles % per_block
    ordered = stacked.at[place].get(mode="promise_in_bounds")
    arrived = lax.all_to_all(ordered, "ia", split_axis=0, concat_axis=0, tiled=True)
    arrived = arrived.reshape(left_count, right_count, tile_width, right_rows * share)
    amp_rows = amplitude_rows(amp_pieces, share)
    sums = pair_sums(arrived, amp_rows, group, right_rows, group_count)
    owned = reduce_to_owner(sums, local_pairs)
    return owned * laplace_factor(pair_list, energy_occupied, energy_left, energy_right)


def solution(mesh):
    sizes = mesh.shape
    cores = 2
    devices = mesh.devices.reshape(sizes["ia"], sizes["ib"] // cores, cores, sizes["op"])
    fine = Mesh(devices, ("ia", "zh", "k", "op"))
    placed = (
        P("ia", ("zh", "k", "op"), None),
        P(None, None, ("zh", "k", "op")),
        P("op", ("ia", "zh", "k"), None),
        P("op", None),
        P(),
        P(),
        P("ia"),
        P(),
    )
    return jax.shard_map(
        per_device, mesh=fine, in_specs=placed, out_specs=P("op", "ia", None), check_vma=False
    )
```

```python
import jax
import jax.numpy as jnp
from jax import lax
from jax.sharding import Mesh
from jax.sharding import PartitionSpec as P
from jax.experimental import pallas as pl
from jax.experimental.pallas import tpu as pltpu


laplace_points = (0.06, 0.25, 0.7, 1.6, 3.5)
laplace_weights = (0.16, 0.36, 0.62, 1.0, 1.7)


def laplace_factor(pair_list, energy_occupied, energy_left, energy_right):
    occupied = energy_occupied.shape[0]
    column = lax.broadcasted_iota(jnp.int32, (pair_list.shape[0], occupied), 1)
    first = jnp.sum(jnp.where(pair_list[:, 0:1] == column, energy_occupied[None, :], 0.0), axis=1)
    second = jnp.sum(jnp.where(pair_list[:, 1:2] == column, energy_occupied[None, :], 0.0), axis=1)
    denominator = (
        energy_left[None, :, None]
        + energy_right[None, None, :]
        - (first + second)[:, None, None]
    )
    factor = jnp.zeros_like(denominator)
    for point, weight in zip(laplace_points, laplace_weights):
        factor = factor + weight * jnp.exp(-point * denominator)
    return factor


def shift(value, axis, step):
    size = lax.axis_size(axis)
    return lax.ppermute(value, axis, [(i, (i + step) % size) for i in range(size)])


def ring_halves(block, axis):
    half = block.shape[0] // 2
    up = shift(block, axis, 1)
    down = shift(block, axis, -1)
    far0 = shift(up[:half], axis, 1)
    far1 = shift(down[half:], axis, -1)
    return [up, down, far0, far1]


def ring_whole(block, axis, step):
    up = shift(block, axis, 1)
    down = shift(block, axis, -1)
    far = shift(up if step > 0 else down, axis, step)
    return [up, down, far]


def ring_split(first, second, axis):
    up0 = shift(first, axis, 1)
    down1 = shift(second, axis, -1)
    up1 = shift(second, axis, 1)
    down0 = shift(first, axis, -1)
    far0 = shift(up0, axis, 1)
    far1 = shift(down1, axis, -1)
    return [up0, up1, down0, down1, far0, far1]


def contract_last(left, right):
    return lax.dot_general(
        left, right, (((1,), (1,)), ((), ())), preferred_element_type=jnp.float32
    )


def group_products(pieces, columns, stacks, kept_shape, sent_shape, row):
    count = len(pieces)
    total = sum(piece.shape[0] for piece in pieces)
    both, depth = columns.shape
    width = both // 2
    step = 1024
    steps = depth // step

    def body(*refs):
        rows, weights = refs[:count], refs[count]
        kept, sent, acc = refs[-3:]
        index = pl.program_id(0)
        left = jnp.concatenate([ref[...] for ref in rows], axis=0)
        product = contract_last(left, weights[:, pl.ds(index * step, step)])

        @pl.when(index == 0)
        def _():
            acc[...] = product

        @pl.when((index > 0) & (index < steps - 1))
        def _():
            acc[...] += product

        @pl.when(index == steps - 1)
        def _():
            result = (acc[...] + product).astype(kept.dtype)
            kept[...] = result[:, :width]
            sent[...] = result[:, width:]

    in_specs = [pl.BlockSpec((piece.shape[0], step), lambda k: (0, k)) for piece in pieces]
    in_specs.append(pl.BlockSpec(memory_space=pltpu.VMEM))
    aliases = {}
    carried = []
    for position, stack in enumerate(stacks):
        if stack is not None:
            aliases[count + 1 + len(carried)] = position
            carried.append(stack)
            in_specs.append(pl.BlockSpec(memory_space=pl.ANY))
    sent_row = row if sent_shape[0] > total else 0
    return pl.pallas_call(
        body,
        grid=(steps,),
        in_specs=in_specs,
        out_specs=[
            pl.BlockSpec((total, width), lambda k: (row, 0)),
            pl.BlockSpec((total, width), lambda k: (sent_row, 0)),
        ],
        out_shape=[
            jax.ShapeDtypeStruct(kept_shape, columns.dtype),
            jax.ShapeDtypeStruct(sent_shape, columns.dtype),
        ],
        scratch_shapes=[pltpu.VMEM((total, both), jnp.float32)],
        input_output_aliases=aliases,
        cost_estimate=pl.CostEstimate(
            flops=2 * total * both * depth,
            transcendentals=0,
            bytes_accessed=2 * depth * (total + both) + 2 * total * both,
        ),
        compiler_params=pltpu.CompilerParams(vmem_limit_bytes=VMEM_LIMIT),
    )(*pieces, pltpu.with_memory_space_constraint(columns, pltpu.VMEM), *carried)


LANE = 128
VMEM_LIMIT = 24 * 1024 * 1024
CHUNK = 16


def lane_window(values, start, share):
    first = start // LANE * LANE
    shift_by = start - first
    low = values[:, first : first + LANE]
    if shift_by == 0:
        return low
    low = pltpu.roll(low, LANE - shift_by, 1)
    if shift_by + share <= LANE:
        return low
    high = pltpu.roll(values[:, first + LANE : first + 2 * LANE], LANE - shift_by, 1)
    place = lax.broadcasted_iota(jnp.int32, low.shape, 1)
    return jnp.where(place < LANE - shift_by, low, high)


def group_slices(amps, group):
    slots, groups, width, lanes = amps.shape

    def body(group_ref, *refs):
        for step in range(groups):
            refs[groups + step][0] = refs[step][0, 0]

    def at(step):
        return lambda i, group_ref: (i, (group_ref[0] + step) & (groups - 1), 0, 0)

    return list(
        pl.pallas_call(
            body,
            grid_spec=pltpu.PrefetchScalarGridSpec(
                num_scalar_prefetch=1,
                grid=(slots,),
                in_specs=[pl.BlockSpec((1, 1, width, lanes), at(step)) for step in range(groups)],
                out_specs=[pl.BlockSpec((1, width, lanes), lambda i, _: (i, 0, 0))] * groups,
            ),
            out_shape=[jax.ShapeDtypeStruct((slots, width, lanes), amps.dtype)] * groups,
            compiler_params=pltpu.CompilerParams(vmem_limit_bytes=VMEM_LIMIT),
            name="txslice",
        )(group.reshape(1), amps, amps, amps, amps)
    )


def amplitude_rows(pieces, share):
    groups = len(pieces)
    slots, width, lanes_in = pieces[0].shape
    local_pairs = lanes_in // share
    chunks = width // CHUNK
    rows = local_pairs * groups * CHUNK

    def body(*refs):
        in_refs, out_ref = refs[:groups], refs[groups]
        for part in range(chunks):
            span = slice(part * CHUNK, (part + 1) * CHUNK)
            block = jnp.concatenate([ref[0, span, :] for ref in in_refs], axis=0)
            block = block.astype(jnp.float32)
            live = lax.broadcasted_iota(jnp.int32, (groups * CHUNK, LANE), 1) < share
            for p in range(local_pairs):
                piece = jnp.where(live, lane_window(block, p * share, share), 0.0)
                out_ref[
                    0,
                    p * groups * CHUNK : (p + 1) * groups * CHUNK,
                    part * LANE : (part + 1) * LANE,
                ] = piece.astype(out_ref.dtype)

    return pl.pallas_call(
        body,
        grid=(slots,),
        in_specs=[pl.BlockSpec((1, width, lanes_in), lambda i: (i, 0, 0))] * groups,
        out_specs=pl.BlockSpec((1, rows, chunks * LANE), lambda i: (i // 2, 0, i % 2)),
        out_shape=jax.ShapeDtypeStruct(
            (slots // 2, rows, 2 * chunks * LANE), pieces[0].dtype
        ),
        compiler_params=pltpu.CompilerParams(vmem_limit_bytes=VMEM_LIMIT),
        name="amprows",
    )(*pieces)


def pair_sums(arrived, amp_rows, group, right_rows, groups):
    left_count, slots, width, _ = arrived.shape
    share = arrived.shape[3] // right_rows
    steps, columns, depth = amp_rows.shape
    local_pairs = columns // (groups * CHUNK)
    chunks = width // CHUNK
    block_rows = left_count * CHUNK
    rows = right_rows * block_rows
    lanes = groups * local_pairs * right_rows

    def body(group_ref, left_ref, right_ref, out_ref, acc):
        index = pl.program_id(0)
        parts = []
        for slot in range(2):
            for part in range(chunks):
                span = slice(part * CHUNK, (part + 1) * CHUNK)
                block = left_ref[:, 2 * index + slot, span, :].astype(jnp.float32)
                block = block.reshape(block_rows, right_rows * share)
                parts.append(
                    jnp.concatenate(
                        [
                            lane_window(block, b * share, share).astype(jnp.bfloat16)
                            for b in range(right_rows)
                        ],
                        axis=0,
                    )
                )
        product = contract_last(jnp.concatenate(parts, axis=1), right_ref[0])

        @pl.when(index == 0)
        def _():
            acc[...] = product

        @pl.when(index > 0)
        def _():
            acc[...] += product

        @pl.when(index == steps - 1)
        def _():
            row_c = lax.broadcasted_iota(jnp.int32, (rows, columns), 0) % CHUNK
            column_c = lax.broadcasted_iota(jnp.int32, (rows, columns), 1) % CHUNK
            diagonal = jnp.where(row_c == column_c, acc[...], 0.0)
            diagonal = jnp.sum(diagonal.reshape(rows // CHUNK, CHUNK, columns), axis=1)
            source = lax.broadcasted_iota(jnp.int32, (columns, lanes), 0) // CHUNK
            target = lax.broadcasted_iota(jnp.int32, (columns, lanes), 1)
            owner = (group_ref[0] + groups - source % groups) % groups
            first = (owner * local_pairs + source // groups) * right_rows
            select = jnp.where(target // right_rows * right_rows == first, 1.0, 0.0)
            spread = jnp.dot(
                diagonal,
                select,
                precision=lax.Precision.HIGHEST,
                preferred_element_type=jnp.float32,
            )
            lane_b = lax.broadcasted_iota(jnp.int32, (left_count, lanes), 1) % right_rows
            total = jnp.zeros((left_count, lanes), jnp.float32)
            for b in range(right_rows):
                mine = spread[b * left_count : (b + 1) * left_count, :]
                total = jnp.where(lane_b == b, mine, total)
            owned = lanes // groups
            for g in range(groups):
                piece = total[:, g * owned : (g + 1) * owned]
                for a in range(left_count):
                    for copy in range(slots):
                        out_ref[(a * slots + copy) * groups + g] = piece[a : a + 1, :]

    return pl.pallas_call(
        body,
        grid_spec=pltpu.PrefetchScalarGridSpec(
            num_scalar_prefetch=1,
            grid=(steps,),
            in_specs=[
                pl.BlockSpec(memory_space=pltpu.VMEM),
                pl.BlockSpec((1, columns, depth), lambda i, _: (i, 0, 0)),
            ],
            out_specs=pl.BlockSpec(
                (left_count * slots * groups, 1, lanes // groups), lambda i, _: (0, 0, 0)
            ),
            scratch_shapes=[pltpu.VMEM((rows, columns), jnp.float32)],
        ),
        out_shape=jax.ShapeDtypeStruct(
            (left_count * slots * groups, 1, lanes // groups), jnp.float32
        ),
        compiler_params=pltpu.CompilerParams(vmem_limit_bytes=VMEM_LIMIT),
        name="pairsums",
    )(group.reshape(1), pltpu.with_memory_space_constraint(arrived, pltpu.VMEM), amp_rows)


def reduce_to_owner(pieces, local_pairs):
    pieces = lax.all_to_all(
        pieces, ("ia", "zh", "k", "op"), split_axis=0, concat_axis=0, tiled=True
    )
    return jnp.sum(pieces, axis=0).reshape(local_pairs, 1, -1)


def per_device(
    fit_coefficients,
    three_center,
    amplitudes,
    pair_list,
    slot_tiles,
    energy_occupied,
    energy_left,
    energy_right,
):
    right_rows = three_center.shape[0]
    share = three_center.shape[2]
    naux = three_center.shape[1]
    tile_width = amplitudes.shape[1]
    local_pairs = amplitudes.shape[0]
    left_count = lax.axis_size("ia")
    high_count = lax.axis_size("zh")
    core_count = lax.axis_size("k")
    group_count = lax.axis_size("op")
    right_count = high_count * core_count
    slot_count = left_count * right_count

    own = fit_coefficients[0]
    rows = own.shape[0]
    below, above, opposite0, opposite1 = ring_halves(own, "zh")
    columns = three_center.transpose(0, 2, 1).reshape(right_rows * share, naux)
    columns_other = shift(columns, "k", 1)
    columns_both = jnp.concatenate([columns, columns_other], axis=0)

    pieces0 = [own] + ring_halves(own, "op")
    pieces1 = [below] + ring_whole(below, "op", 1)
    pieces1 += [above] + ring_whole(above, "op", -1)
    pieces2 = [opposite0, opposite1] + ring_split(opposite0, opposite1, "op")

    split_amps = amplitudes.reshape(local_pairs, tile_width, right_count, group_count, share)
    split_amps = split_amps.transpose(2, 3, 1, 0, 4)
    split_amps = split_amps.reshape(right_count, group_count, tile_width, local_pairs * share)
    amps = lax.all_to_all(
        split_amps, ("zh", "k"), split_axis=0, concat_axis=0, tiled=True
    )
    group = lax.axis_index("op")

    amp_pieces = group_slices(amps, group)
    for step in range(1, group_count):
        amp_pieces[step] = shift(amp_pieces[step], "op", step)

    ring = group_count * rows
    kept_shape = (high_count * ring, right_rows * share)
    first_shape = (high_count * ring - rows, right_rows * share)
    last_shape = (rows, right_rows * share)
    kept, sent = group_products(pieces0, columns_both, (None, None), kept_shape, first_shape, 2)
    kept, sent = group_products(pieces1, columns_both, (kept, sent), kept_shape, first_shape, 0)
    kept, sent = group_products(
        pieces2[:-2], columns_both, (kept, sent), kept_shape, first_shape, 4
    )
    kept, sent_last = group_products(
        pieces2[-2:], columns_both, (kept, None), kept_shape, last_shape, 15
    )
    swapped = [shift(sent, "k", 1), shift(sent_last, "k", 1)]
    stacked = jnp.concatenate([kept] + swapped, axis=0)
    stacked = stacked.reshape(slot_count, tile_width, right_rows * share)

    per_block = rows // tile_width
    block_of = slot_tiles // per_block
    step = (block_of % group_count - lax.axis_index("op")) % group_count
    across = jnp.where(step == 0, 0, jnp.where(step == 3, 1, step + 1))
    core = (block_of // group_count) % core_count
    step = (block_of // (group_count * core_count) - lax.axis_index("zh")) % high_count
    up = jnp.where(step == 0, 2, jnp.where(step == 3, 0, jnp.where(step == 1, 1, 3)))
    swap = jnp.where(core == lax.axis_index("k"), 0, high_count)
    place = ((swap + up) * group_count + across) * per_block + slot_tiles % per_block
    ordered = stacked.at[place].get(mode="promise_in_bounds")
    arrived = lax.all_to_all(ordered, "ia", split_axis=0, concat_axis=0, tiled=True)
    arrived = arrived.reshape(left_count, right_count, tile_width, right_rows * share)
    amp_rows = amplitude_rows(amp_pieces, share)
    sums = pair_sums(arrived, amp_rows, group, right_rows, group_count)
    owned = reduce_to_owner(sums, local_pairs)
    return owned * laplace_factor(pair_list, energy_occupied, energy_left, energy_right)


def solution(mesh):
    sizes = mesh.shape
    cores = 2
    devices = mesh.devices.reshape(sizes["ia"], sizes["ib"] // cores, cores, sizes["op"])
    fine = Mesh(devices, ("ia", "zh", "k", "op"))
    placed = (
        P("ia", ("zh", "k", "op"), None),
        P(None, None, ("zh", "k", "op")),
        P("op", ("ia", "zh", "k"), None),
        P("op", None),
        P(),
        P(),
        P("ia"),
        P(),
    )
    return jax.shard_map(
        per_device, mesh=fine, in_specs=placed, out_specs=P("op", "ia", None), check_vma=False
    )
```

```python
import jax
import jax.numpy as jnp
from jax import lax
from jax.sharding import Mesh
from jax.sharding import PartitionSpec as P
from jax.experimental import pallas as pl
from jax.experimental.pallas import tpu as pltpu


laplace_points = (0.06, 0.25, 0.7, 1.6, 3.5)
laplace_weights = (0.16, 0.36, 0.62, 1.0, 1.7)


def laplace_factor(pair_list, energy_occupied, energy_left, energy_right):
    occupied = energy_occupied.shape[0]
    column = lax.broadcasted_iota(jnp.int32, (pair_list.shape[0], occupied), 1)
    first = jnp.sum(jnp.where(pair_list[:, 0:1] == column, energy_occupied[None, :], 0.0), axis=1)
    second = jnp.sum(jnp.where(pair_list[:, 1:2] == column, energy_occupied[None, :], 0.0), axis=1)
    denominator = (
        energy_left[None, :, None]
        + energy_right[None, None, :]
        - (first + second)[:, None, None]
    )
    factor = jnp.zeros_like(denominator)
    for point, weight in zip(laplace_points, laplace_weights):
        factor = factor + weight * jnp.exp(-point * denominator)
    return factor


def shift(value, axis, step):
    size = lax.axis_size(axis)
    return lax.ppermute(value, axis, [(i, (i + step) % size) for i in range(size)])


def ring_halves(block, axis):
    half = block.shape[0] // 2
    up = shift(block, axis, 1)
    down = shift(block, axis, -1)
    far0 = shift(up[:half], axis, 1)
    far1 = shift(down[half:], axis, -1)
    return [up, down, far0, far1]


def ring_whole(block, axis, step):
    up = shift(block, axis, 1)
    down = shift(block, axis, -1)
    far = shift(up if step > 0 else down, axis, step)
    return [up, down, far]


def ring_split(first, second, axis):
    up0 = shift(first, axis, 1)
    down1 = shift(second, axis, -1)
    up1 = shift(second, axis, 1)
    down0 = shift(first, axis, -1)
    far0 = shift(up0, axis, 1)
    far1 = shift(down1, axis, -1)
    return [up0, up1, down0, down1, far0, far1]


def contract_last(left, right):
    return lax.dot_general(
        left, right, (((1,), (1,)), ((), ())), preferred_element_type=jnp.float32
    )


def group_products(pieces, columns, stacks, kept_shape, sent_shape, row):
    count = len(pieces)
    total = sum(piece.shape[0] for piece in pieces)
    both, depth = columns.shape
    width = both // 2
    step = 1024
    steps = depth // step

    def body(*refs):
        rows, weights = refs[:count], refs[count]
        kept, sent, acc = refs[-3:]
        index = pl.program_id(0)
        left = jnp.concatenate([ref[...] for ref in rows], axis=0)
        product = contract_last(left, weights[...])

        @pl.when(index == 0)
        def _():
            acc[...] = product

        @pl.when((index > 0) & (index < steps - 1))
        def _():
            acc[...] += product

        @pl.when(index == steps - 1)
        def _():
            result = (acc[...] + product).astype(kept.dtype)
            kept[...] = result[:, :width]
            sent[...] = result[:, width:]

    in_specs = [pl.BlockSpec((piece.shape[0], step), lambda k: (0, k)) for piece in pieces]
    in_specs.append(pl.BlockSpec((both, step), lambda k: (0, k)))
    aliases = {}
    carried = []
    for position, stack in enumerate(stacks):
        if stack is not None:
            aliases[count + 1 + len(carried)] = position
            carried.append(stack)
            in_specs.append(pl.BlockSpec(memory_space=pl.ANY))
    sent_row = row if sent_shape[0] > total else 0
    return pl.pallas_call(
        body,
        grid=(steps,),
        in_specs=in_specs,
        out_specs=[
            pl.BlockSpec((total, width), lambda k: (row, 0)),
            pl.BlockSpec((total, width), lambda k: (sent_row, 0)),
        ],
        out_shape=[
            jax.ShapeDtypeStruct(kept_shape, columns.dtype),
            jax.ShapeDtypeStruct(sent_shape, columns.dtype),
        ],
        scratch_shapes=[pltpu.VMEM((total, both), jnp.float32)],
        input_output_aliases=aliases,
        cost_estimate=pl.CostEstimate(
            flops=2 * total * both * depth,
            transcendentals=0,
            bytes_accessed=2 * depth * (total + both) + 2 * total * both,
        ),
    )(*pieces, columns, *carried)


LANE = 128
VMEM_LIMIT = 24 * 1024 * 1024
CHUNK = 16


def lane_window(values, start, share):
    first = start // LANE * LANE
    shift_by = start - first
    low = values[:, first : first + LANE]
    if shift_by == 0:
        return low
    low = pltpu.roll(low, LANE - shift_by, 1)
    if shift_by + share <= LANE:
        return low
    high = pltpu.roll(values[:, first + LANE : first + 2 * LANE], LANE - shift_by, 1)
    place = lax.broadcasted_iota(jnp.int32, low.shape, 1)
    return jnp.where(place < LANE - shift_by, low, high)


def amplitude_rows(pieces, share):
    groups = len(pieces)
    slots, width, lanes_in = pieces[0].shape
    local_pairs = lanes_in // share
    chunks = width // CHUNK
    rows = local_pairs * groups * CHUNK

    def body(*refs):
        in_refs, out_ref = refs[:groups], refs[groups]
        for part in range(chunks):
            span = slice(part * CHUNK, (part + 1) * CHUNK)
            block = jnp.concatenate([ref[0, span, :] for ref in in_refs], axis=0)
            live = lax.broadcasted_iota(jnp.int32, (groups * CHUNK, LANE), 1) < share
            for p in range(local_pairs):
                piece = jnp.where(live, lane_window(block, p * share, share), 0.0)
                out_ref[
                    0,
                    p * groups * CHUNK : (p + 1) * groups * CHUNK,
                    part * LANE : (part + 1) * LANE,
                ] = piece.astype(out_ref.dtype)

    return pl.pallas_call(
        body,
        grid=(slots,),
        in_specs=[pl.BlockSpec((1, width, lanes_in), lambda i: (i, 0, 0))] * groups,
        out_specs=pl.BlockSpec((1, rows, chunks * LANE), lambda i: (i // 2, 0, i % 2)),
        out_shape=jax.ShapeDtypeStruct(
            (slots // 2, rows, 2 * chunks * LANE), pieces[0].dtype
        ),
        name="amprows",
    )(*pieces)


def pair_sums(arrived, amp_rows, group, right_rows, groups):
    left_count, slots, width, _ = arrived.shape
    share = arrived.shape[3] // right_rows
    steps, columns, depth = amp_rows.shape
    local_pairs = columns // (groups * CHUNK)
    chunks = width // CHUNK
    block_rows = left_count * CHUNK
    rows = right_rows * block_rows
    lanes = groups * local_pairs * right_rows

    def body(group_ref, left_ref, right_ref, out_ref, acc):
        index = pl.program_id(0)
        parts = []
        for slot in range(2):
            for part in range(chunks):
                span = slice(part * CHUNK, (part + 1) * CHUNK)
                block = left_ref[:, 2 * index + slot, span, :]
                block = block.reshape(block_rows, right_rows * share)
                parts.append(
                    jnp.concatenate(
                        [
                            lane_window(block, b * share, share).astype(jnp.bfloat16)
                            for b in range(right_rows)
                        ],
                        axis=0,
                    )
                )
        product = contract_last(jnp.concatenate(parts, axis=1), right_ref[0])

        @pl.when(index == 0)
        def _():
            acc[...] = product

        @pl.when(index > 0)
        def _():
            acc[...] += product

        @pl.when(index == steps - 1)
        def _():
            row_c = lax.broadcasted_iota(jnp.int32, (rows, columns), 0) % CHUNK
            column_c = lax.broadcasted_iota(jnp.int32, (rows, columns), 1) % CHUNK
            diagonal = jnp.where(row_c == column_c, acc[...], 0.0)
            diagonal = jnp.sum(diagonal.reshape(rows // CHUNK, CHUNK, columns), axis=1)
            source = lax.broadcasted_iota(jnp.int32, (columns, lanes), 0) // CHUNK
            target = lax.broadcasted_iota(jnp.int32, (columns, lanes), 1)
            owner = (group_ref[0] + groups - source % groups) % groups
            first = (owner * local_pairs + source // groups) * right_rows
            select = jnp.where(target // right_rows * right_rows == first, 1.0, 0.0)
            spread = jnp.dot(
                diagonal,
                select,
                precision=lax.Precision.HIGHEST,
                preferred_element_type=jnp.float32,
            )
            lane_b = lax.broadcasted_iota(jnp.int32, (left_count, lanes), 1) % right_rows
            total = jnp.zeros((left_count, lanes), jnp.float32)
            for b in range(right_rows):
                mine = spread[b * left_count : (b + 1) * left_count, :]
                total = jnp.where(lane_b == b, mine, total)
            owned = lanes // groups
            for g in range(groups):
                piece = total[:, g * owned : (g + 1) * owned]
                for a in range(left_count):
                    for copy in range(slots):
                        out_ref[(a * slots + copy) * groups + g] = piece[a : a + 1, :]

    return pl.pallas_call(
        body,
        grid_spec=pltpu.PrefetchScalarGridSpec(
            num_scalar_prefetch=1,
            grid=(steps,),
            in_specs=[
                pl.BlockSpec(memory_space=pltpu.VMEM),
                pl.BlockSpec((1, columns, depth), lambda i, _: (i, 0, 0)),
            ],
            out_specs=pl.BlockSpec(
                (left_count * slots * groups, 1, lanes // groups), lambda i, _: (0, 0, 0)
            ),
            scratch_shapes=[pltpu.VMEM((rows, columns), jnp.float32)],
        ),
        out_shape=jax.ShapeDtypeStruct(
            (left_count * slots * groups, 1, lanes // groups), jnp.float32
        ),
        compiler_params=pltpu.CompilerParams(vmem_limit_bytes=VMEM_LIMIT),
        name="pairsums",
    )(group.reshape(1), pltpu.with_memory_space_constraint(arrived, pltpu.VMEM), pltpu.with_memory_space_constraint(amp_rows, pltpu.HBM))


def reduce_to_owner(pieces, local_pairs):
    pieces = lax.all_to_all(
        pieces, ("ia", "zh", "k", "op"), split_axis=0, concat_axis=0, tiled=True
    )
    return jnp.sum(pieces, axis=0).reshape(local_pairs, 1, -1)


def per_device(
    fit_coefficients,
    three_center,
    amplitudes,
    pair_list,
    slot_tiles,
    energy_occupied,
    energy_left,
    energy_right,
):
    right_rows = three_center.shape[0]
    share = three_center.shape[2]
    naux = three_center.shape[1]
    tile_width = amplitudes.shape[1]
    local_pairs = amplitudes.shape[0]
    left_count = lax.axis_size("ia")
    high_count = lax.axis_size("zh")
    core_count = lax.axis_size("k")
    group_count = lax.axis_size("op")
    right_count = high_count * core_count
    slot_count = left_count * right_count

    own = fit_coefficients[0]
    rows = own.shape[0]
    below, above, opposite0, opposite1 = ring_halves(own, "zh")
    columns = three_center.transpose(0, 2, 1).reshape(right_rows * share, naux)
    columns_other = shift(columns, "k", 1)
    columns_both = jnp.concatenate([columns, columns_other], axis=0)

    pieces0 = [own] + ring_halves(own, "op")
    pieces1 = [below] + ring_whole(below, "op", 1)
    pieces1 += [above] + ring_whole(above, "op", -1)
    pieces2 = [opposite0, opposite1] + ring_split(opposite0, opposite1, "op")

    split_amps = amplitudes.reshape(local_pairs, tile_width, right_count, group_count, share)
    split_amps = split_amps.transpose(2, 3, 1, 0, 4)
    split_amps = split_amps.reshape(right_count, group_count, tile_width, local_pairs * share)
    amps = lax.all_to_all(
        split_amps, ("zh", "k"), split_axis=0, concat_axis=0, tiled=True
    )
    group = lax.axis_index("op")

    def for_step(step):
        to = (group + step) & (group_count - 1)
        return lax.dynamic_index_in_dim(amps, to, axis=1, keepdims=False)

    amp_pieces = [for_step(0)]
    for step in range(1, group_count):
        amp_pieces.append(shift(for_step(step), "op", step))

    ring = group_count * rows
    kept_shape = (high_count * ring, right_rows * share)
    first_shape = (high_count * ring - rows, right_rows * share)
    last_shape = (rows, right_rows * share)
    kept, sent = group_products(pieces0, columns_both, (None, None), kept_shape, first_shape, 2)
    kept, sent = group_products(pieces1, columns_both, (kept, sent), kept_shape, first_shape, 0)
    kept, sent = group_products(
        pieces2[:-2], columns_both, (kept, sent), kept_shape, first_shape, 4
    )
    kept, sent_last = group_products(
        pieces2[-2:], columns_both, (kept, None), kept_shape, last_shape, 15
    )
    swapped = [shift(sent, "k", 1), shift(sent_last, "k", 1)]
    stacked = jnp.concatenate([kept] + swapped, axis=0)
    stacked = stacked.reshape(slot_count, tile_width, right_rows * share)

    per_block = rows // tile_width
    block_of = slot_tiles // per_block
    step = (block_of % group_count - lax.axis_index("op")) % group_count
    across = jnp.where(step == 0, 0, jnp.where(step == 3, 1, step + 1))
    core = (block_of // group_count) % core_count
    step = (block_of // (group_count * core_count) - lax.axis_index("zh")) % high_count
    up = jnp.where(step == 0, 2, jnp.where(step == 3, 0, jnp.where(step == 1, 1, 3)))
    swap = jnp.where(core == lax.axis_index("k"), 0, high_count)
    place = ((swap + up) * group_count + across) * per_block + slot_tiles % per_block
    ordered = stacked.at[place].get(mode="promise_in_bounds")
    arrived = lax.all_to_all(ordered, "ia", split_axis=0, concat_axis=0, tiled=True)
    arrived = arrived.reshape(left_count, right_count, tile_width, right_rows * share)
    amp_rows = amplitude_rows(amp_pieces, share)
    sums = pair_sums(arrived, amp_rows, group, right_rows, group_count)
    owned = reduce_to_owner(sums, local_pairs)
    return owned * laplace_factor(pair_list, energy_occupied, energy_left, energy_right)


def solution(mesh):
    sizes = mesh.shape
    cores = 2
    devices = mesh.devices.reshape(sizes["ia"], sizes["ib"] // cores, cores, sizes["op"])
    fine = Mesh(devices, ("ia", "zh", "k", "op"))
    placed = (
        P("ia", ("zh", "k", "op"), None),
        P(None, None, ("zh", "k", "op")),
        P("op", ("ia", "zh", "k"), None),
        P("op", None),
        P(),
        P(),
        P("ia"),
        P(),
    )
    return jax.shard_map(
        per_device, mesh=fine, in_specs=placed, out_specs=P("op", "ia", None), check_vma=False
    )
```
